32 devices in a mesh: fsdp: 8 (over z, x), tp: 4 (over y, core).
Axes of the slice: x: 2, y: 2, z: 4, core: 2. Of those that a mesh axis runs over, the one named last changes fastest.
Arguments:
- tokens: bfloat16 [8192, 1024], P(('fsdp', 'tp')), may hold values from -6 to 6
- lengths: int32 [4], replicated, may hold values from 1 to 4096, 8192 in all
- attn_gain: bfloat16 [1024], P('fsdp'), may hold values from 0.5 to 1.5
- w_query: bfloat16 [1024, 1024], P('fsdp', 'tp'), may hold values from -0.1875 to 0.1875
- w_key: bfloat16 [1024, 1024], P('fsdp', 'tp'), may hold values from -0.1875 to 0.1875
- w_value: bfloat16 [1024, 2048], P('fsdp', 'tp'), may hold values from -0.1875 to 0.1875
- w_gate_out: bfloat16 [1024, 2048], P('fsdp', 'tp'), may hold values from -0.1875 to 0.1875
- w_beta: bfloat16 [1024, 8], P('fsdp', 'tp'), may hold values from -0.1875 to 0.1875
- w_decay: bfloat16 [1024, 8], P('fsdp', 'tp'), may hold values from -0.1875 to 0.1875
- conv_query: bfloat16 [4, 8, 128], P(None, 'tp', 'fsdp'), may hold values from -2.5 to 2.5
- conv_key: bfloat16 [4, 8, 128], P(None, 'tp', 'fsdp'), may hold values from -2.5 to 2.5
- conv_value: bfloat16 [4, 8, 256], P(None, 'tp', 'fsdp'), may hold values from -2.5 to 2.5
- decay_log: float32 [8], P('tp'), may hold values from -6 to -1
- decay_bias: float32 [8], P('tp'), may hold values from -1.5 to 0.5
- out_gain: bfloat16 [256], P('fsdp'), may hold values from 0.5 to 1.5
- w_out: bfloat16 [2048, 1024], P('tp', 'fsdp'), may hold values from -0.25 to 0.25
- ffn_gain: bfloat16 [1024], P('fsdp'), may hold values from 0.5 to 1.5
- w_ffn_gate: bfloat16 [1024, 2816], P('fsdp', 'tp'), may hold values from -0.1875 to 0.1875
- w_ffn_up: bfloat16 [1024, 2816], P('fsdp', 'tp'), may hold values from -0.1875 to 0.1875
- w_ffn_down: bfloat16 [2816, 1024], P('tp', 'fsdp'), may hold values from -0.21875 to 0.21875
- cotangent: bfloat16 [8192, 1024], P(('fsdp', 'tp')), may hold values from -6 to 6
Outputs:
- output: float32 [8192, 1024], P(('fsdp', 'tp'))
- d_tokens: float32 [8192, 1024], P(('fsdp', 'tp'))
- grad_attn_gain: float32 [1024], P('fsdp')
- grad_w_query: float32 [1024, 1024], P('fsdp', 'tp')
- grad_w_key: float32 [1024, 1024], P('fsdp', 'tp')
- grad_w_value: float32 [1024, 2048], P('fsdp', 'tp')
- grad_w_gate_out: float32 [1024, 2048], P('fsdp', 'tp')
- grad_w_beta: float32 [1024, 8], P('fsdp', 'tp')
- grad_w_decay: float32 [1024, 8], P('fsdp', 'tp')
- grad_conv_query: float32 [4, 8, 128], P(None, 'tp', 'fsdp')
- grad_conv_key: float32 [4, 8, 128], P(None, 'tp', 'fsdp')
- grad_conv_value: float32 [4, 8, 256], P(None, 'tp', 'fsdp')
- grad_decay_log: float32 [8], P('tp')
- grad_decay_bias: float32 [8], P('tp')
- grad_out_gain: float32 [256], P('fsdp')
- grad_w_out: float32 [2048, 1024], P('tp', 'fsdp')
- grad_ffn_gain: float32 [1024], P('fsdp')
- grad_w_ffn_gate: float32 [1024, 2816], P('fsdp', 'tp')
- grad_w_ffn_up: float32 [1024, 2816], P('fsdp', 'tp')
- grad_w_ffn_down: float32 [2816, 1024], P('tp', 'fsdp')
The draws below stay inside these ranges and needn't reach their ends.
Inputs may be any that keep to these rules, and one draw needn't show every extreme that they name: The 4 lengths sum to 8192; the largest is exactly 4096.
All inputs are finite; a program needn't handle non-finite values.
Results may differ from the reference program's by a relative error of at most 0.03.
Values may be sent and summed in bfloat16 or wider, within the bound.
A program may use at most 256 MiB of HBM per device.

```python
import math
import jax
import jax.numpy as jnp
import numpy as np
from jax import lax

D = 1024
H = 8
K = 128
V = 256
FF = 2816
CONV = 4
GROUP = 64
MAXLEN = 4096
TOKENS = 8192
NSEQ = 4


def shard_levels(rng, shape, cuts, low, high):
    gain = 1.0
    for position, parts in cuts:
        heights = jax.random.uniform(jax.random.fold_in(jax.random.fold_in(rng, 6), position), (parts,), jnp.float32, low / len(cuts), high / len(cuts))
        gain = gain * jnp.repeat(jnp.exp(heights), shape[position] // parts).reshape((-1,) + (1,) * (len(shape) - 1 - position))
    return gain


def split_up(count, total, bound, slope):
    portions = [(1 << 20) // math.isqrt(rank ** slope) + 1 for rank in range(2, count + 1)]
    surplus, counts = total - bound - (count - 1), [1] * (count - 1)
    while surplus > 0:
        movable = [i for i in range(count - 1) if counts[i] < bound]
        pool, left = sum([portions[i] for i in movable]), surplus
        for i in movable:
            addition = min(bound - counts[i], max(1, left * portions[i] // pool), surplus)
            counts[i] = counts[i] + addition
            surplus = surplus - addition
    return np.array([bound] + counts)


def ragged_sizes(stream_key, amount, total, limit, slope):
    if amount == 2:
        one = jax.random.randint(stream_key, (), max(1, total - limit), min(limit, total - 1) + 1)
        return jnp.stack([one, total - one])
    tallies = jnp.asarray(split_up(amount, total, limit, slope), jnp.int32)
    pairs = (amount - 1) // 2
    donor, receiver = tallies[1:1 + 2 * pairs:2], tallies[2:2 + 2 * pairs:2]
    margin = jnp.minimum(donor - 1, limit - receiver)
    moved = jax.random.randint(jax.random.fold_in(stream_key, 1), (pairs,), 0, 1 << 20) % (margin + 1)
    tallies = tallies.at[1:1 + 2 * pairs:2].set(donor - moved).at[2:2 + 2 * pairs:2].set(receiver + moved)
    return tallies[jax.random.permutation(jax.random.fold_in(stream_key, 2), amount)]


def scatter_about(rng, shape, scale, limit, cuts=(), kind=jnp.bfloat16):
    gain = shard_levels(rng, shape, cuts, -0.22, 0.18) if cuts else 1.0
    array = jax.random.normal(rng, shape, jnp.float32) * scale * gain
    return jnp.minimum(jnp.maximum(array, -limit), limit).astype(kind)


def setup_inputs(seed: int = 0) -> dict:
    arg_keys = jax.random.split(jax.random.key(seed), 22)
    tokens = scatter_about(arg_keys[0], (TOKENS, D), 1.0, 6.0, ((0, 32),))
    lengths = ragged_sizes(arg_keys[1], NSEQ, TOKENS, MAXLEN, 2).astype(jnp.int32)
    attn_gain = jnp.clip(1.0 + 0.1 * jax.random.normal(arg_keys[2], (D,), jnp.float32), 0.5, 1.5).astype(jnp.bfloat16)
    w_query = scatter_about(arg_keys[3], (D, H * K), D ** -0.5, 0.1875, ((0, 8), (1, 4)))
    w_key = scatter_about(arg_keys[4], (D, H * K), D ** -0.5, 0.1875, ((0, 8), (1, 4)))
    w_value = scatter_about(arg_keys[5], (D, H * V), D ** -0.5, 0.1875, ((0, 8), (1, 4)))
    w_gate_out = scatter_about(arg_keys[6], (D, H * V), D ** -0.5, 0.1875, ((0, 8), (1, 4)))
    w_beta = scatter_about(arg_keys[7], (D, H), D ** -0.5, 0.1875, ((0, 8), (1, 4)))
    w_decay = scatter_about(arg_keys[8], (D, H), D ** -0.5, 0.1875, ((0, 8), (1, 4)))
    conv_query = scatter_about(arg_keys[9], (CONV, H, K), 0.5, 2.5, ((1, 4), (2, 8)))
    conv_key = scatter_about(arg_keys[10], (CONV, H, K), 0.5, 2.5, ((1, 4), (2, 8)))
    conv_value = scatter_about(arg_keys[11], (CONV, H, V), 0.5, 2.5, ((1, 4), (2, 8)))
    decay_log = jnp.clip(-6.0 + 5.0 * jax.random.uniform(arg_keys[12], (H,), jnp.float32) ** shard_levels(arg_keys[12], (H,), ((0, 4),), -0.2, 0.2), -6.0, -1.0)
    decay_bias = jnp.clip(-1.5 + 2.0 * jax.random.uniform(arg_keys[13], (H,), jnp.float32) ** shard_levels(arg_keys[13], (H,), ((0, 4),), -0.2, 0.2), -1.5, 0.5)
    out_gain = jnp.clip(1.0 + 0.1 * jax.random.normal(arg_keys[14], (V,), jnp.float32), 0.5, 1.5).astype(jnp.bfloat16)
    w_out = scatter_about(arg_keys[15], (H * V, D), (H * V // 4) ** -0.5, 0.25, ((0, 4), (1, 8)))
    ffn_gain = jnp.clip(1.0 + 0.1 * jax.random.normal(arg_keys[16], (D,), jnp.float32), 0.5, 1.5).astype(jnp.bfloat16)
    w_ffn_gate = scatter_about(arg_keys[17], (D, FF), D ** -0.5, 0.1875, ((0, 8), (1, 4)))
    w_ffn_up = scatter_about(arg_keys[18], (D, FF), D ** -0.5, 0.1875, ((0, 8), (1, 4)))
    w_ffn_down = scatter_about(arg_keys[19], (FF, D), (FF // 4) ** -0.5, 0.21875, ((0, 4), (1, 8)))
    cotangent = scatter_about(arg_keys[20], (TOKENS, D), 1.0, 6.0, ((0, 32),))
    return {"tokens": tokens, "lengths": lengths, "attn_gain": attn_gain, "w_query": w_query, "w_key": w_key, "w_value": w_value, "w_gate_out": w_gate_out, "w_beta": w_beta, "w_decay": w_decay, "conv_query": conv_query, "conv_key": conv_key, "conv_value": conv_value, "decay_log": decay_log, "decay_bias": decay_bias, "out_gain": out_gain, "w_out": w_out, "ffn_gain": ffn_gain, "w_ffn_gate": w_ffn_gate, "w_ffn_up": w_ffn_up, "w_ffn_down": w_ffn_down, "cotangent": cotangent}


highest = lax.Precision.HIGHEST

def mat_dot(left, right):
    return jnp.dot(left.astype(jnp.float32), right.astype(jnp.float32), preferred_element_type=jnp.float32)

def rms_scale(values, scale_gain):
    return values * lax.rsqrt(lax.optimization_barrier(jnp.mean(values * values, axis=-1, keepdims=True)) + 1e-06) * scale_gain

def unit_rows(values):
    return values * lax.rsqrt(lax.optimization_barrier(jnp.sum(values * values, axis=-1, keepdims=True)) + 1e-06)

def seq_begin(lengths, positions):
    offsets = (jnp.cumsum(lengths) - lengths).astype(jnp.int32)
    chosen = jnp.where(offsets[None, :] <= positions[:, None], offsets[None, :], 0)
    return lax.optimization_barrier(jnp.max(chosen, axis=1)).astype(jnp.int32)

def split_heads(flat, width):
    return flat.reshape(flat.shape[0], -1, width).transpose(1, 0, 2)

def merge_heads(stacked):
    return stacked.transpose(1, 0, 2).reshape(stacked.shape[1], -1)

def short_conv(inputs, rim_rows, kernel, begins, positions):
    row_count = inputs.shape[0]
    padded = jnp.concatenate([rim_rows, inputs], axis=0)
    result = kernel[0] * inputs
    for lag_step in range(1, CONV):
        in_range = (positions - lag_step >= begins).astype(inputs.dtype)[:, None]
        start_row = CONV - 1 - lag_step
        result = result + kernel[lag_step] * padded[start_row:start_row + row_count] * in_range
    return jax.nn.silu(result)

def head_inputs(query_raw, key_raw, value_raw, query_rim, key_rim, value_rim, query_kernel, key_kernel, value_kernel, beta_raw, decay_raw, decay_scale, decay_shift, begins, positions):
    query_vec = unit_rows(short_conv(query_raw, query_rim, query_kernel, begins, positions)) * query_raw.shape[1] ** (-0.5)
    key_vec = unit_rows(short_conv(key_raw, key_rim, key_kernel, begins, positions))
    value_vec = short_conv(value_raw, value_rim, value_kernel, begins, positions)
    beta_gate = jax.nn.sigmoid(beta_raw)
    decay_rate = -jnp.exp(decay_scale) * jax.nn.softplus(decay_raw + decay_shift)
    return (query_vec, key_vec, value_vec, beta_gate, decay_rate)

def block_terms(query_vec, key_vec, value_vec, beta_gate, decay_rate, begins, positions):
    blocks = query_vec.shape[0] // GROUP
    query_block = query_vec.reshape(blocks, GROUP, -1)
    key_block = key_vec.reshape(blocks, GROUP, -1)
    value_block = value_vec.reshape(blocks, GROUP, -1)
    beta_block = beta_gate.reshape(blocks, GROUP)
    decay_block = decay_rate.reshape(blocks, GROUP)
    begin_block = begins.reshape(blocks, GROUP)
    place_block = positions.reshape(blocks, GROUP)
    cumul = jnp.cumsum(decay_block, axis=1)
    same_seq = (begin_block[:, :, None] <= place_block[:, None, :]) & (place_block[:, None, :] <= place_block[:, :, None])
    same_float = same_seq.astype(query_vec.dtype)
    factor = jnp.exp(jnp.where(same_seq, cumul[:, :, None] - cumul[:, None, :], 0.0)) * same_float
    alive_mask = (begin_block < place_block[:, :1]).astype(query_vec.dtype)
    carry_scale = jnp.exp(cumul) * alive_mask
    strict = (place_block[:, None, :] < place_block[:, :, None]).astype(query_vec.dtype)
    key_gram = jnp.einsum('ntd,nsd->nts', key_block, key_block, precision=highest)
    lower_mat = jnp.eye(GROUP, dtype=query_vec.dtype)[None] + beta_block[:, :, None] * key_gram * factor * strict
    value_part = lax.linalg.triangular_solve(lower_mat, beta_block[:, :, None] * value_block, left_side=True, lower=True, unit_diagonal=True)
    key_part = lax.linalg.triangular_solve(lower_mat, (beta_block * carry_scale)[:, :, None] * key_block, left_side=True, lower=True, unit_diagonal=True)
    scores = jnp.einsum('ntd,nsd->nts', query_block, key_block, precision=highest) * factor
    key_last = key_block * factor[:, -1, :, None]
    return (query_block, carry_scale, scores, value_part, key_part, key_last)

def mixer_head(query_raw, key_raw, value_raw, query_kernel, key_kernel, value_kernel, beta_raw, decay_raw, decay_scale, decay_shift, gate_raw, out_scale, begins, positions):
    query_rim = jnp.zeros((CONV - 1, query_raw.shape[1]), query_raw.dtype)
    key_rim = jnp.zeros((CONV - 1, key_raw.shape[1]), key_raw.dtype)
    value_rim = jnp.zeros((CONV - 1, value_raw.shape[1]), value_raw.dtype)
    inputs = head_inputs(query_raw, key_raw, value_raw, query_rim, key_rim, value_rim, query_kernel, key_kernel, value_kernel, beta_raw, decay_raw, decay_scale, decay_shift, begins, positions)
    block_parts = block_terms(*inputs, begins, positions)

    def advance(state_now, pieces):
        query_block, scale_block, score_block, value_block, key_block, last_block = pieces
        update = value_block - jnp.dot(key_block, state_now, precision=highest)
        result = scale_block[:, None] * jnp.dot(query_block, state_now, precision=highest) + jnp.dot(score_block, update, precision=highest)
        state_now = scale_block[-1] * state_now + jnp.dot(last_block.T, update, precision=highest)
        return (state_now, result)
    start_state = jnp.zeros((key_raw.shape[1], value_raw.shape[1]), query_raw.dtype)
    _, results = lax.scan(advance, start_state, block_parts)
    outputs = results.reshape(-1, value_raw.shape[1])
    return rms_scale(outputs, out_scale) * jax.nn.silu(gate_raw)

def reference(tokens, lengths, attn_gain, w_query, w_key, w_value, w_gate_out, w_beta, w_decay, conv_query, conv_key, conv_value, decay_log, decay_bias, out_gain, w_out, ffn_gain, w_ffn_gate, w_ffn_up, w_ffn_down, cotangent):
    row_count = tokens.shape[0]
    positions = jnp.arange(row_count, dtype=jnp.int32)
    begins = seq_begin(lengths, positions)
    rows_float = tokens.astype(jnp.float32)
    normed_attn, pull_attn = jax.vjp(rms_scale, rows_float, attn_gain.astype(jnp.float32))
    normed_attn = normed_attn.astype(jnp.bfloat16)
    proj_query = mat_dot(normed_attn, w_query).astype(jnp.bfloat16)
    proj_key = mat_dot(normed_attn, w_key).astype(jnp.bfloat16)
    proj_value = mat_dot(normed_attn, w_value).astype(jnp.bfloat16)
    gate_raw = mat_dot(normed_attn, w_gate_out)
    beta_raw = mat_dot(normed_attn, w_beta)
    decay_raw = mat_dot(normed_attn, w_decay)
    out_scale = out_gain.astype(jnp.float32)
    head_items = (split_heads(proj_query.astype(jnp.float32), K), split_heads(proj_key.astype(jnp.float32), K), split_heads(proj_value.astype(jnp.float32), V), jnp.transpose(conv_query.astype(jnp.float32), (1, 0, 2)), jnp.transpose(conv_key.astype(jnp.float32), (1, 0, 2)), jnp.transpose(conv_value.astype(jnp.float32), (1, 0, 2)), beta_raw.T, decay_raw.T, decay_log, decay_bias, split_heads(gate_raw, V))

    def head_forward(items):
        return mixer_head(*items, out_scale, begins, positions)
    mixer_out = lax.map(head_forward, head_items)
    normed_mixer = merge_heads(mixer_out).astype(jnp.bfloat16)
    hidden = rows_float + mat_dot(normed_mixer, w_out)
    normed_ffn, pull_ffn = jax.vjp(rms_scale, hidden, ffn_gain.astype(jnp.float32))
    normed_ffn = normed_ffn.astype(jnp.bfloat16)
    gate_pre = mat_dot(normed_ffn, w_ffn_gate)
    up_pre = mat_dot(normed_ffn, w_ffn_up)
    gate_sigmoid = jax.nn.sigmoid(gate_pre)
    activated = (gate_pre * gate_sigmoid * up_pre).astype(jnp.bfloat16)
    output = hidden + mat_dot(activated, w_ffn_down)
    d_active = mat_dot(cotangent, w_ffn_down.T)
    grad_w_ffn_down = mat_dot(activated.T, cotangent)
    d_gate = (d_active * up_pre * gate_sigmoid * (1.0 + gate_pre * (1.0 - gate_sigmoid))).astype(jnp.bfloat16)
    d_upper = (d_active * gate_pre * gate_sigmoid).astype(jnp.bfloat16)
    grad_w_ffn_gate = mat_dot(normed_ffn.T, d_gate)
    grad_w_ffn_up = mat_dot(normed_ffn.T, d_upper)
    d_normed_ffn = mat_dot(d_gate, w_ffn_gate.T) + mat_dot(d_upper, w_ffn_up.T)
    d_hidden_norm, grad_ffn_gain = pull_ffn(d_normed_ffn)
    d_hidden = cotangent.astype(jnp.float32) + d_hidden_norm
    d_hidden_half = d_hidden.astype(jnp.bfloat16)
    d_mixer = mat_dot(d_hidden_half, w_out.T)
    grad_w_out = mat_dot(normed_mixer.T, d_hidden_half)

    def head_backward(items):
        primal = items[:11]

        def local_head(*head_args):
            return mixer_head(*head_args, begins, positions)
        _, pull_head = jax.vjp(local_head, *primal, out_scale)
        return pull_head(items[11])
    head_grads = lax.map(head_backward, head_items + (split_heads(d_mixer, V),))
    d_query_half = merge_heads(head_grads[0]).astype(jnp.bfloat16)
    d_key_half = merge_heads(head_grads[1]).astype(jnp.bfloat16)
    d_value_half = merge_heads(head_grads[2]).astype(jnp.bfloat16)
    d_gate_half = merge_heads(head_grads[10]).astype(jnp.bfloat16)
    d_beta_half = head_grads[6].T.astype(jnp.bfloat16)
    d_decay_half = head_grads[7].T.astype(jnp.bfloat16)
    grad_conv_query = jnp.transpose(head_grads[3], (1, 0, 2))
    grad_conv_key = jnp.transpose(head_grads[4], (1, 0, 2))
    grad_conv_value = jnp.transpose(head_grads[5], (1, 0, 2))
    grad_decay_log = head_grads[8]
    grad_decay_bias = head_grads[9]
    grad_out_gain = lax.optimization_barrier(jnp.sum(head_grads[11], axis=0))
    grad_w_query = mat_dot(normed_attn.T, d_query_half)
    grad_w_key = mat_dot(normed_attn.T, d_key_half)
    grad_w_value = mat_dot(normed_attn.T, d_value_half)
    grad_w_gate_out = mat_dot(normed_attn.T, d_gate_half)
    grad_w_beta = mat_dot(normed_attn.T, d_beta_half)
    grad_w_decay = mat_dot(normed_attn.T, d_decay_half)
    d_normed_attn = mat_dot(d_query_half, w_query.T) + mat_dot(d_key_half, w_key.T) + mat_dot(d_value_half, w_value.T) + mat_dot(d_gate_half, w_gate_out.T) + mat_dot(d_beta_half, w_beta.T) + mat_dot(d_decay_half, w_decay.T)
    d_rows_norm, grad_attn_gain = pull_attn(d_normed_attn)
    d_tokens = d_hidden + d_rows_norm
    return (output, d_tokens, grad_attn_gain, grad_w_query, grad_w_key, grad_w_value, grad_w_gate_out, grad_w_beta, grad_w_decay, grad_conv_query, grad_conv_key, grad_conv_value, grad_decay_log, grad_decay_bias, grad_out_gain, grad_w_out, grad_ffn_gain, grad_w_ffn_gate, grad_w_ffn_up, grad_w_ffn_down)
```

```python
import jax
import jax.numpy as jnp
from jax import lax
from jax.sharding import PartitionSpec as P

K = 128
V = 256
CONV = 4
GROUP = 128
MAXLEN = 4096


highest = lax.Precision.HIGHEST
high = lax.Precision.HIGH


def shifted(array, axis, by):
    count = lax.axis_size(axis)
    pairs = [(i, i + by) for i in range(count) if 0 <= i + by < count]
    return lax.ppermute(array, axis, pairs)


def mat_dot(left, right):
    return jnp.dot(left, right, preferred_element_type=jnp.float32)


def rms_scale(values, scale_gain):
    return (
        values * lax.rsqrt(jnp.mean(values * values, axis=-1, keepdims=True) + 1e-06) * scale_gain
    )


def unit_rows(values):
    return values * lax.rsqrt(jnp.sum(values * values, axis=-1, keepdims=True) + 1e-06)


def seq_begin(lengths, positions):
    offsets = jnp.cumsum(lengths) - lengths
    chosen = jnp.where(offsets[None, :] <= positions[:, None], offsets[None, :], 0)
    return jnp.max(chosen, axis=1)


def split_heads(flat, width):
    return flat.reshape(flat.shape[0], -1, width).transpose(1, 0, 2)


def merge_heads(stacked):
    return stacked.transpose(1, 0, 2).reshape(stacked.shape[1], -1)


def short_conv(inputs, rim_rows, kernel, begins, positions):
    row_count = inputs.shape[0]
    padded = jnp.concatenate([rim_rows, inputs], axis=0)
    result = kernel[0] * inputs
    for lag_step in range(1, CONV):
        in_range = (positions - lag_step >= begins).astype(inputs.dtype)[:, None]
        start_row = CONV - 1 - lag_step
        result = result + kernel[lag_step] * padded[start_row : start_row + row_count] * in_range
    return jax.nn.silu(result)


def head_inputs(
    query_raw,
    key_raw,
    value_raw,
    query_rim,
    key_rim,
    value_rim,
    query_kernel,
    key_kernel,
    value_kernel,
    beta_raw,
    decay_raw,
    decay_scale,
    decay_shift,
    begins,
    positions,
):
    query_vec = unit_rows(
        short_conv(query_raw, query_rim, query_kernel, begins, positions)
    ) * query_raw.shape[1] ** (-0.5)
    key_vec = unit_rows(short_conv(key_raw, key_rim, key_kernel, begins, positions))
    value_vec = short_conv(value_raw, value_rim, value_kernel, begins, positions)
    beta_gate = jax.nn.sigmoid(beta_raw)
    decay_rate = -jnp.exp(decay_scale) * jax.nn.softplus(decay_raw + decay_shift)
    return (query_vec, key_vec, value_vec, beta_gate, decay_rate)


def level_mask(size, step):
    row = lax.broadcasted_iota(jnp.int32, (size, size), 0) // step
    col = lax.broadcasted_iota(jnp.int32, (size, size), 1) // step
    return ((row // 2 == col // 2) & (row > col)).astype(jnp.float32)


@jax.custom_vjp
def unit_lower_inverse(strict_lower):
    size = strict_lower.shape[-1]
    inverse = jnp.eye(size, dtype=strict_lower.dtype) - strict_lower * level_mask(size, 1)
    step = 2
    while step < size:
        corner = strict_lower * level_mask(size, step)
        inverse = inverse - jnp.matmul(
            jnp.matmul(inverse, corner, precision=high), inverse, precision=high
        )
        step = step * 2
    return inverse


def unit_lower_inverse_fwd(strict_lower):
    inverse = unit_lower_inverse(strict_lower)
    return inverse, inverse


def unit_lower_inverse_bwd(inverse, grad):
    flipped = jnp.swapaxes(inverse, -1, -2)
    return (-jnp.matmul(jnp.matmul(flipped, grad, precision=high), flipped, precision=high),)


unit_lower_inverse.defvjp(unit_lower_inverse_fwd, unit_lower_inverse_bwd)


def block_terms(query_vec, key_vec, value_vec, beta_gate, decay_rate, begins, positions):
    blocks = query_vec.shape[0] // GROUP
    query_block = query_vec.reshape(blocks, GROUP, -1)
    key_block = key_vec.reshape(blocks, GROUP, -1)
    value_block = value_vec.reshape(blocks, GROUP, -1)
    beta_block = beta_gate.reshape(blocks, GROUP)
    decay_block = decay_rate.reshape(blocks, GROUP)
    begin_block = begins.reshape(blocks, GROUP)
    place_block = positions.reshape(blocks, GROUP)
    upper = jnp.triu(jnp.ones((GROUP, GROUP), decay_block.dtype))
    cumul = jnp.dot(decay_block, upper, precision=highest)
    same_seq = (begin_block[:, :, None] <= place_block[:, None, :]) & (
        place_block[:, None, :] <= place_block[:, :, None]
    )
    same_float = same_seq.astype(query_vec.dtype)
    factor = jnp.exp(jnp.where(same_seq, cumul[:, :, None] - cumul[:, None, :], 0.0)) * same_float
    alive_mask = (begin_block < place_block[:, :1]).astype(query_vec.dtype)
    carry_scale = jnp.exp(cumul) * alive_mask
    strict = (place_block[:, None, :] < place_block[:, :, None]).astype(query_vec.dtype)
    key_gram = jnp.einsum("ntd,nsd->nts", key_block, key_block, precision=high)
    inverse = unit_lower_inverse(beta_block[:, :, None] * key_gram * factor * strict)
    value_part = jnp.matmul(inverse, beta_block[:, :, None] * value_block)
    key_part = jnp.matmul(inverse, (beta_block * carry_scale)[:, :, None] * key_block)
    scores = jnp.einsum("ntd,nsd->nts", query_block, key_block) * factor
    key_last = key_block * factor[:, -1, :, None]
    return (query_block, carry_scale, scores, value_part, key_part, key_last)


def state_maps(block_parts):
    _, carry_scale, _, value_part, key_part, key_last = block_parts
    maps = jnp.einsum("hncj,hnck->hnjk", key_last, key_part)
    offsets = jnp.einsum("hncj,hncv->hnjv", key_last, value_part)
    return carry_scale[:, :, -1][:, :, None, None], maps, offsets


def state_run(scales, maps, offsets):
    heads, blocks = maps.shape[:2]
    matrix = jnp.broadcast_to(jnp.eye(K, dtype=jnp.float32), (heads, K, K))
    pair = jnp.concatenate([matrix, jnp.zeros_like(offsets[:, 0])], axis=-1)
    drive = jnp.concatenate([jnp.zeros_like(maps), offsets], axis=-1)
    starts = []
    for block in range(blocks):
        starts.append(pair)
        pair = (
            scales[:, block] * pair
            + drive[:, block]
            - jnp.einsum("hij,hjv->hiv", maps[:, block], pair, precision=high)
        )
    return jnp.stack(starts, axis=1), pair


def adjoint_run(scales, maps, local_grads, last):
    blocks = maps.shape[1]
    after = [None] * blocks
    grad = last
    for block in reversed(range(blocks)):
        after[block] = grad
        grad = (
            scales[:, block] * grad
            + local_grads[:, block]
            - jnp.einsum("hji,hjv->hiv", maps[:, block], grad, precision=high)
        )
    return jnp.stack(after, axis=1), grad


def entering(pairs, axis, row_count):
    count, mine = (lax.axis_size(axis), lax.axis_index(axis))
    hops = min(count - 1, -(-MAXLEN // row_count))
    state = jnp.zeros_like(pairs[0][..., K:])
    for hop in range(hops, 0, -1):
        piece = lax.dynamic_index_in_dim(pairs, jnp.maximum(mine - hop, 0), 0, False)
        new = (
            jnp.einsum("hij,hjv->hiv", piece[..., :K], state, precision=high) + piece[..., K:]
        )
        state = jnp.where(mine >= hop, new, state)
    return state


def carried_in(pairs, grads, axis, row_count):
    count, mine = (lax.axis_size(axis), lax.axis_index(axis))
    hops = min(count - 1, -(-MAXLEN // row_count))
    grad = jnp.zeros(grads.shape[1:], jnp.float32)
    for hop in range(hops, 0, -1):
        source = jnp.minimum(mine + hop, count - 1)
        piece = lax.dynamic_index_in_dim(pairs, source, 0, False)
        own = lax.dynamic_index_in_dim(grads, source, 0, False).astype(jnp.float32)
        new = jnp.einsum("hji,hjv->hiv", piece[..., :K], grad, precision=high) + own
        grad = jnp.where(mine + hop < count, new, grad)
    return grad


def step_states(block_parts, start_states):
    _, carry_scale, _, value_part, key_part, key_last = block_parts
    update = value_part - jnp.einsum("hncj,hnjv->hncv", key_part, start_states)
    return carry_scale[:, :, -1][:, :, None, None] * start_states + jnp.einsum(
        "hncj,hncv->hnjv", key_last, update
    )


def front_all(
    mixed_raw,
    rim_raw,
    query_kernel,
    key_kernel,
    value_kernel,
    beta_raw,
    decay_raw,
    decay_scale,
    decay_shift,
    begins,
    positions,
    head_count,
):
    query_width = head_count * K

    def front_one_head(
        query_raw,
        key_raw,
        value_raw,
        query_rim,
        key_rim,
        value_rim,
        query_taps,
        key_taps,
        value_taps,
        beta_head,
        decay_head,
        scale_head,
        shift_head,
    ):
        inputs = head_inputs(
            query_raw,
            key_raw,
            value_raw,
            query_rim,
            key_rim,
            value_rim,
            query_taps,
            key_taps,
            value_taps,
            beta_head,
            decay_head,
            scale_head,
            shift_head,
            begins,
            positions,
        )
        return block_terms(*inputs, begins, positions)

    return jax.vmap(front_one_head)(
        split_heads(mixed_raw[:, :query_width], K),
        split_heads(mixed_raw[:, query_width : 2 * query_width], K),
        split_heads(mixed_raw[:, 2 * query_width :], V),
        split_heads(rim_raw[:, :query_width], K),
        split_heads(rim_raw[:, query_width : 2 * query_width], K),
        split_heads(rim_raw[:, 2 * query_width :], V),
        jnp.transpose(query_kernel, (1, 0, 2)),
        jnp.transpose(key_kernel, (1, 0, 2)),
        jnp.transpose(value_kernel, (1, 0, 2)),
        beta_raw.T,
        decay_raw.T,
        decay_scale,
        decay_shift,
    )


def back_all(block_parts, start_states, gate_heads, out_scale):
    query_block, carry_scale, scores, value_part, key_part, _ = block_parts
    update = value_part - jnp.einsum("hncj,hnjv->hncv", key_part, start_states)
    outputs = carry_scale[..., None] * jnp.einsum("hncj,hnjv->hncv", query_block, start_states)
    outputs = outputs + jnp.einsum("hnts,hnsv->hntv", scores, update)
    outputs = outputs.reshape(outputs.shape[0], -1, outputs.shape[-1])
    return rms_scale(outputs, out_scale) * jax.nn.silu(gate_heads)


def shards(
    tokens,
    lengths,
    attn_gain,
    w_query,
    w_key,
    w_value,
    w_gate_out,
    w_beta,
    w_decay,
    conv_query,
    conv_key,
    conv_value,
    decay_log,
    decay_bias,
    out_gain,
    w_out,
    ffn_gain,
    w_ffn_gate,
    w_ffn_up,
    w_ffn_down,
    cotangent,
):
    count = lax.axis_size("fsdp")
    shard_rows = tokens.shape[0]
    query_cols, value_cols = w_query.shape[1], w_value.shape[1]
    hidden_cols = w_ffn_gate.shape[1]
    head_count = query_cols // K
    mixed_cols = 2 * query_cols + value_cols
    raw_cols = mixed_cols + value_cols

    own_float = tokens.astype(jnp.float32)
    small = jnp.concatenate(
        [
            part.reshape(-1)
            for part in (attn_gain, ffn_gain, out_gain, conv_query, conv_key, conv_value)
        ]
    )
    small = lax.all_gather(small, "fsdp")
    smalls, at = ([], 0)
    for part in (attn_gain, ffn_gain, out_gain, conv_query, conv_key, conv_value):
        piece = small[:, at : at + part.size].astype(jnp.float32)
        at = at + part.size
        if part.ndim == 3:
            piece = piece.reshape((count,) + part.shape).transpose(1, 2, 0, 3)
            smalls.append(piece.reshape(part.shape[0], part.shape[1], -1))
        else:
            smalls.append(piece.reshape(-1))
    gain_one, gain_two, norm_out, query_taps, key_taps, value_taps = smalls
    mixer_w = lax.all_gather(
        jnp.concatenate([w_query, w_key, w_value, w_gate_out, w_beta, w_decay], axis=1),
        "fsdp",
        axis=0,
        tiled=True,
    )
    out_t = lax.all_gather(w_out.T, "fsdp", axis=0, tiled=True)
    ffn_gate_w = lax.all_gather(w_ffn_gate, "fsdp", axis=0, tiled=True)
    ffn_up_w = lax.all_gather(w_ffn_up, "fsdp", axis=0, tiled=True)
    down_t = lax.all_gather(w_ffn_down.T, "fsdp", axis=0, tiled=True)
    normed_one_own, pull_one = jax.vjp(rms_scale, own_float, gain_one)
    normed_one = lax.all_gather(
        normed_one_own.astype(jnp.bfloat16), "tp", axis=0, tiled=True
    )
    cot_rows = lax.all_gather(cotangent, "tp", axis=0, tiled=True)
    row_count = normed_one.shape[0]
    positions = lax.axis_index("fsdp") * row_count + jnp.arange(row_count, dtype=jnp.int32)
    begins = seq_begin(lengths, positions)
    raw = mat_dot(normed_one, mixer_w)
    mixed_raw = raw[:, :mixed_cols].astype(jnp.bfloat16)
    gate_raw = raw[:, mixed_cols:raw_cols]
    beta_raw = raw[:, raw_cols : raw_cols + head_count]
    decay_raw = raw[:, raw_cols + head_count :]
    rim_recv = shifted(mixed_raw[row_count - (CONV - 1) :], "fsdp", 1)

    def front_local(*inputs):
        return front_all(*inputs, begins, positions, head_count)

    block_parts, pull_front = jax.vjp(
        front_local,
        mixed_raw.astype(jnp.float32),
        rim_recv.astype(jnp.float32),
        query_taps,
        key_taps,
        value_taps,
        beta_raw,
        decay_raw,
        decay_log,
        decay_bias,
    )
    scales, maps, offsets = state_maps(block_parts)
    prefixes, final_pair = state_run(scales, maps, offsets)
    pairs = lax.all_gather(final_pair, "fsdp")
    state_in = entering(pairs, "fsdp", row_count)
    start_states = (
        jnp.einsum("hnij,hjv->hniv", prefixes[..., :K], state_in, precision=high)
        + prefixes[..., K:]
    )
    mixer_out, pull_back = jax.vjp(
        back_all, block_parts, start_states, split_heads(gate_raw, V), norm_out
    )
    normed_mixer = merge_heads(mixer_out).astype(jnp.bfloat16)
    mixer_part = lax.dot_general(
        normed_mixer, out_t, (((1,), (1,)), ((), ())), preferred_element_type=jnp.float32
    )
    mixer_own = lax.psum_scatter(
        mixer_part.astype(jnp.bfloat16), "tp", scatter_dimension=0, tiled=True
    ).astype(jnp.float32)
    hidden_own = own_float + mixer_own
    normed_two_own, pull_two = jax.vjp(rms_scale, hidden_own, gain_two)
    normed_two = lax.all_gather(
        normed_two_own.astype(jnp.bfloat16), "tp", axis=0, tiled=True
    )
    gate_pre = mat_dot(normed_two, ffn_gate_w)
    up_pre = mat_dot(normed_two, ffn_up_w)
    gate_sigmoid = jax.nn.sigmoid(gate_pre)
    activated = (gate_pre * gate_sigmoid * up_pre).astype(jnp.bfloat16)
    d_active = mat_dot(cot_rows, down_t)
    d_gate = (d_active * up_pre * gate_sigmoid * (1.0 + gate_pre * (1.0 - gate_sigmoid))).astype(
        jnp.bfloat16
    )
    d_upper = (d_active * gate_pre * gate_sigmoid).astype(jnp.bfloat16)
    d_normed_two = mat_dot(d_gate, ffn_gate_w.T) + mat_dot(d_upper, ffn_up_w.T)
    d_normed_two_own = lax.psum_scatter(
        d_normed_two.astype(jnp.bfloat16), "tp", scatter_dimension=0, tiled=True
    ).astype(jnp.float32)
    d_hidden_norm, gain_two_part = pull_two(d_normed_two_own)
    d_hidden = cotangent.astype(jnp.float32) + d_hidden_norm
    d_hidden_rows = lax.all_gather(d_hidden.astype(jnp.bfloat16), "tp", axis=0, tiled=True)
    ffn_part = mat_dot(activated, down_t.T)
    ffn_own = lax.psum_scatter(
        ffn_part.astype(jnp.bfloat16), "tp", scatter_dimension=0, tiled=True
    ).astype(jnp.float32)
    output = hidden_own + ffn_own

    def summed(grad):
        return lax.psum_scatter(
            grad.astype(jnp.bfloat16), "fsdp", scatter_dimension=0, tiled=True
        ).astype(jnp.float32)

    grad_w_ffn_gate = summed(mat_dot(normed_two.T, d_gate))
    grad_w_ffn_up = summed(mat_dot(normed_two.T, d_upper))
    grad_w_ffn_down = summed(mat_dot(cot_rows.T, activated)).T
    d_mixer = mat_dot(d_hidden_rows, out_t)
    grad_w_out = summed(mat_dot(d_hidden_rows.T, normed_mixer)).T
    d_parts, d_starts, d_gate_heads, norm_out_part = pull_back(split_heads(d_mixer, V))
    _, d_state_in = adjoint_run(scales, maps, d_starts, jnp.zeros_like(state_in))
    d_state_out = carried_in(
        pairs, lax.all_gather(d_state_in.astype(jnp.bfloat16), "fsdp"), "fsdp", row_count
    )
    d_next, _ = adjoint_run(scales, maps, d_starts, d_state_out)
    _, pull_step = jax.vjp(lambda parts: step_states(parts, start_states), block_parts)
    d_parts = jax.tree.map(jnp.add, d_parts, pull_step(d_next)[0])
    (
        d_mixed,
        d_rim,
        d_query_taps,
        d_key_taps,
        d_value_taps,
        d_beta_raw,
        d_decay_raw,
        d_decay_log,
        d_decay_bias,
    ) = pull_front(d_parts)
    rim_grad = shifted(d_rim, "fsdp", -1)
    d_mixed = d_mixed.at[row_count - (CONV - 1) :].add(rim_grad)
    d_raw = jnp.concatenate(
        [
            part.astype(jnp.bfloat16)
            for part in (d_mixed, merge_heads(d_gate_heads), d_beta_raw, d_decay_raw)
        ],
        axis=1,
    )
    d_normed_one = mat_dot(d_raw, mixer_w.T)
    d_normed_one_own = lax.psum_scatter(
        d_normed_one.astype(jnp.bfloat16), "tp", scatter_dimension=0, tiled=True
    ).astype(jnp.float32)
    d_rows_norm, gain_one_part = pull_one(d_normed_one_own)
    d_tokens = d_hidden + d_rows_norm
    grad_mixer_w = summed(mat_dot(normed_one.T, d_raw))
    cuts = (
        query_cols,
        2 * query_cols,
        mixed_cols,
        raw_cols,
        raw_cols + head_count,
    )
    grads_w = jnp.split(grad_mixer_w, cuts, axis=1)
    gains = lax.psum(jnp.concatenate([gain_one_part, gain_two_part, norm_out_part]), "tp")
    width = gain_one.shape[0]

    def spread(taps):
        taps = taps.reshape(taps.shape[0], taps.shape[1], count, -1)
        return taps.transpose(2, 0, 1, 3).reshape(count, -1)

    decay_pair = jnp.concatenate([d_decay_log, d_decay_bias])
    small_parts = [
        gains[:width].reshape(count, -1),
        gains[width : 2 * width].reshape(count, -1),
        gains[2 * width :].reshape(count, -1),
        spread(d_query_taps),
        spread(d_key_taps),
        spread(d_value_taps),
        jnp.broadcast_to(decay_pair[None, :], (count, decay_pair.shape[0])),
    ]
    small_sum = lax.psum_scatter(
        jnp.concatenate(small_parts, axis=1), "fsdp", scatter_dimension=0, tiled=True
    )[0]
    small_cuts, at = ([], 0)
    for part in small_parts[:-1]:
        at = at + part.shape[1]
        small_cuts.append(at)
    small_out = jnp.split(small_sum, small_cuts)
    return (
        output,
        d_tokens,
        small_out[0],
        *grads_w,
        small_out[3].reshape(conv_query.shape),
        small_out[4].reshape(conv_key.shape),
        small_out[5].reshape(conv_value.shape),
        small_out[6][:head_count],
        small_out[6][head_count:],
        small_out[2],
        grad_w_out,
        small_out[1],
        grad_w_ffn_gate,
        grad_w_ffn_up,
        grad_w_ffn_down,
    )


def solution(mesh):
    placed = (
        P(("fsdp", "tp"), None),
        P(),
        P("fsdp"),
        P("fsdp", "tp"),
        P("fsdp", "tp"),
        P("fsdp", "tp"),
        P("fsdp", "tp"),
        P("fsdp", "tp"),
        P("fsdp", "tp"),
        P(None, "tp", "fsdp"),
        P(None, "tp", "fsdp"),
        P(None, "tp", "fsdp"),
        P("tp"),
        P("tp"),
        P("fsdp"),
        P("tp", "fsdp"),
        P("fsdp"),
        P("fsdp", "tp"),
        P("fsdp", "tp"),
        P("tp", "fsdp"),
        P(("fsdp", "tp"), None),
    )
    return jax.shard_map(
        shards,
        mesh=mesh,
        in_specs=placed,
        out_specs=(
            P(("fsdp", "tp"), None),
            P(("fsdp", "tp"), None),
            P("fsdp"),
            P("fsdp", "tp"),
            P("fsdp", "tp"),
            P("fsdp", "tp"),
            P("fsdp", "tp"),
            P("fsdp", "tp"),
            P("fsdp", "tp"),
            P(None, "tp", "fsdp"),
            P(None, "tp", "fsdp"),
            P(None, "tp", "fsdp"),
            P("tp"),
            P("tp"),
            P("fsdp"),
            P("tp", "fsdp"),
            P("fsdp"),
            P("fsdp", "tp"),
            P("fsdp", "tp"),
            P("tp", "fsdp"),
        ),
        check_vma=False,
    )
```
